128 devices in a mesh: island: 8 (over z, x_lo), fsdp: 16 (over x_hi, y, core).
Axes of the slice: x: 4 (x_hi: 2, x_lo: 2; x = x_hi * 2 + x_lo), y: 4, z: 4, core: 2. Of those that a mesh axis runs over, the one named last changes fastest.
Arguments:
- tokens: bfloat16 [8, 8192, 8192], P('island', 'fsdp'), may hold values from -6 to 6
- key_grad_out: bfloat16 [8, 8192, 1024], P('island', 'fsdp'), may hold values from -0.0625 to 0.0625
- key_master: float32 [8, 8192, 1024], P('island', 'fsdp'), may hold values from -0.0625 to 0.0625
- key_first: float32 [8, 8192, 1024], P('island', 'fsdp'), may hold values from -4 to 4
- key_second: float32 [8, 8192, 1024], P('island', 'fsdp'), may hold values from 0.05 to 2
- frag_local: float32 [8, 8192, 1024], P('island', 'fsdp'), may hold values from -1.5 to 1.5
- frag_anchor: float32 [8192, 1024], P('fsdp'), may hold values from -1.5 to 1.5
- frag_momentum: float32 [8192, 1024], P('fsdp'), may hold values from -1.5 to 1.5
Outputs:
- new_master: float32 [8, 8192, 1024], P('island', 'fsdp')
- new_first: float32 [8, 8192, 1024], P('island', 'fsdp')
- new_second: float32 [8, 8192, 1024], P('island', 'fsdp')
- next_keys: float32 [8, 8192, 1024], P('island', 'fsdp')
- new_anchor: float32 [8192, 1024], P('fsdp')
- new_momentum: float32 [8192, 1024], P('fsdp')
The draws below stay inside these ranges and needn't reach their ends.
All inputs are finite; a program needn't handle non-finite values.
Results may differ from the reference program's by a relative error of at most 0.0029.
Values may be sent and summed in bfloat16 or wider, within the bound.
No kernel may reach another device: no remote copies, remote signals or barrier semaphores. Data moves between devices by JAX's collectives and lax.ppermute only.
A program may use at most 192 MiB of HBM per device.

```python
import math
import jax
import jax.numpy as jnp
from jax import lax

D = 8192
KV = 1024
TOKENS = 8192
N_ISLAND = 8


def raised(drawn, rng, source, target, shards_of, factor):
    def block_of(position):
        return (jnp.arange(drawn.shape[position]) // (drawn.shape[position] // shards_of)).reshape((-1,) + (1,) * (drawn.ndim - 1 - position))

    one_side = jax.random.permutation(rng, shards_of)[block_of(target)]
    other_side = (block_of(target) + shards_of // 2) % shards_of
    return jnp.where((block_of(source) == one_side) | (block_of(source) == other_side), factor * drawn, drawn)


def shard_levels(key, extent, shards, least, high):
    factor_of = 1.0
    for axis_at, blocks in shards:
        heights = jax.random.uniform(jax.random.fold_in(jax.random.fold_in(key, 6), axis_at), (blocks,), jnp.float32, least / len(shards), high / len(shards))
        factor_of = factor_of * jnp.repeat(jnp.exp(heights), extent[axis_at] // blocks).reshape((-1,) + (1,) * (len(extent) - 1 - axis_at))
    return factor_of


def noise(own_key, dims, spread, reach, shards=(), kind=jnp.bfloat16):
    level = shard_levels(own_key, dims, shards, -0.22, 0.18) if shards else 1.0
    values = jax.random.normal(own_key, dims, jnp.float32) * spread * level
    return jnp.minimum(jnp.maximum(values, -reach), reach).astype(kind)


def heavy_noise(own_key, dims, spread, reach, cuts, heavy, kind=jnp.bfloat16):
    drawn = spread * jax.random.normal(own_key, dims, jnp.float32)
    if cuts:
        drawn = drawn * shard_levels(own_key, dims, cuts, -0.22, 0.18)
    return jnp.clip(raised(drawn, jax.random.fold_in(own_key, 3), *heavy), -reach, reach).astype(kind)


def setup_inputs(seed: int = 0) -> dict:
    arg_keys = jax.random.split(jax.random.key(seed), 9)
    return {
        "tokens": heavy_noise(arg_keys[0], (N_ISLAND, TOKENS, D), 1.0, 6.0, ((0, 8), (1, 16)), (1, 2, 16, 2.0)),
        "key_grad_out": noise(arg_keys[1], (N_ISLAND, TOKENS, KV), TOKENS ** -0.5, 0.0625, ((0, 8), (1, 16))),
        "key_master": noise(arg_keys[2], (N_ISLAND, D, KV), D ** -0.5, 0.0625, ((0, 8), (1, 16)), jnp.float32),
        "key_first": noise(arg_keys[3], (N_ISLAND, D, KV), 0.3, 4.0, ((0, 8), (1, 16)), jnp.float32),
        "key_second": jnp.clip(jnp.exp(math.log(2.0) - 3.6888794 * jax.random.uniform(arg_keys[4], (N_ISLAND, D, KV), jnp.float32) ** shard_levels(arg_keys[4], (N_ISLAND, D, KV), ((0, 8), (1, 16)), -0.2, 0.2)), 0.05, 2.0),
        "frag_local": noise(arg_keys[5], (N_ISLAND, D, KV), 0.1, 1.5, ((0, 8), (1, 16)), jnp.float32),
        "frag_anchor": noise(arg_keys[6], (D, KV), 0.1, 1.5, ((0, 16),), jnp.float32),
        "frag_momentum": noise(arg_keys[7], (D, KV), 0.1, 1.5, ((0, 16),), jnp.float32),
    }


BETA_ONE = 0.9
BETA_TWO = 0.95
INNER_RATE = 0.002
DECAY_RATE = 0.1
EPSILON = 1e-08
OUTER_RATE = 0.7
OUTER_MOMENT = 0.9

def reference(tokens, key_grad_out, key_master, key_first, key_second, frag_local, frag_anchor, frag_momentum):
    masters = []
    firsts = []
    seconds = []
    keys_all = []
    for island_num in range(N_ISLAND):
        activations = tokens[island_num]
        upstream = key_grad_out[island_num]
        grad = lax.dot_general(activations, upstream, (((0,), (0,)), ((), ())), preferred_element_type=jnp.float32)
        first_new = BETA_ONE * key_first[island_num] + (1.0 - BETA_ONE) * grad
        second_new = BETA_TWO * key_second[island_num] + (1.0 - BETA_TWO) * grad * grad
        update = first_new / (jnp.sqrt(second_new) + EPSILON)
        master_new = key_master[island_num] - INNER_RATE * (update + DECAY_RATE * key_master[island_num])
        weight_bf = master_new.astype(jnp.bfloat16)
        keys_all.append(jnp.dot(activations, weight_bf, preferred_element_type=jnp.float32))
        masters.append(master_new)
        firsts.append(first_new)
        seconds.append(second_new)
    total = lax.optimization_barrier(jnp.sum(frag_anchor[None] - frag_local, axis=0))
    outer_grad = total / N_ISLAND
    new_momentum = OUTER_MOMENT * frag_momentum + outer_grad
    new_anchor = frag_anchor - OUTER_RATE * (outer_grad + OUTER_MOMENT * new_momentum)
    return (jnp.stack(masters), jnp.stack(firsts), jnp.stack(seconds), jnp.stack(keys_all), new_anchor, new_momentum)
```

```python
import jax
import jax.numpy as jnp
from jax import lax
from jax.sharding import PartitionSpec as P

BETA_ONE = 0.9
BETA_TWO = 0.95
INNER_RATE = 0.002
DECAY_RATE = 0.1
EPSILON = 1e-08
OUTER_RATE = 0.7
OUTER_MOMENT = 0.9

BF = jnp.bfloat16
F32 = jnp.float32

N_Y = 4
N_FSDP = 16
SPLIT = 512


def place(x_hi, y, core):
    return (x_hi % 2) * 8 + (y % N_Y) * 2 + core % 2


def moves(d_x, d_y, d_core):
    pairs = []
    for index in range(N_FSDP):
        x_hi, y, core = index // 8, (index // 2) % N_Y, index % 2
        pairs.append((index, place(x_hi + d_x, y + d_y, core + d_core)))
    return pairs


SWAP = moves(0, 0, 1)
ACROSS = moves(1, 0, 0)
UP = moves(0, 1, 0)
DOWN = moves(0, -1, 0)
Z_GROUPS = [[2 * z + x_lo for z in range(4)] for x_lo in range(2)]
X_LO = [(i, i ^ 1) for i in range(8)]


def send(value, pairs):
    return lax.ppermute(value, "fsdp", pairs)


def outer_update(outer_grad, anchor_rows, momentum_rows):
    momentum_new = OUTER_MOMENT * momentum_rows + outer_grad
    anchor_new = anchor_rows - OUTER_RATE * (outer_grad + OUTER_MOMENT * momentum_new)
    return (anchor_new, momentum_new)


def grad_term(features, upstream):
    return lax.dot_general(
        features, upstream, (((0,), (0,)), ((), ())), preferred_element_type=F32
    )


class Line:
    def __init__(self):
        self.mark = ()

    def step(self, *values):
        out = lax.optimization_barrier((*values, *self.mark))[: len(values)]
        self.mark = tuple(out)
        return out[0] if len(values) == 1 else out


def per_device(
    tokens, key_grad_out, key_master, key_first, key_second, frag_local, frag_anchor, frag_momentum
):
    me = lax.axis_index("fsdp")
    x_hi, y, core = me // 8, (me // 2) % N_Y, me % 2
    activations = tokens[0]
    upstream = key_grad_out[0]
    count, width = activations.shape
    rows = width // N_FSDP
    half = rows // 2
    line = Line()

    def columns(r, which_core):
        return jnp.concatenate(
            [
                lax.dynamic_slice(
                    activations, (0, place(x_hi + p, y + r, which_core) * rows), (count, rows)
                )
                for p in range(2)
            ],
            axis=1,
        )

    def term_a(r):
        return grad_term(features[r], up_a).reshape(2, rows, SPLIT)

    def term_b(r, p):
        return grad_term(features[r][:, p * rows : (p + 1) * rows], up_b)

    other_up = send(upstream, SWAP)
    far_sent = line.step(columns(2, 1 - core))
    far_got = send(far_sent, SWAP)
    activations, other_up, far_got = line.step(activations, other_up, far_got)
    upstream_all = jnp.concatenate([upstream, other_up], axis=0)
    up_a, up_b = upstream_all[:, :SPLIT], upstream_all[:, SPLIT:]
    features = {2: jnp.concatenate([columns(2, core), far_got], axis=0)}

    a_far = term_a(2).astype(BF)
    b_far = term_b(2, 1).astype(BF)
    a_far, b_far, activations = line.step(a_far, b_far, activations)
    a_low, a_high = send(a_far[:, :half], UP), send(a_far[:, half:], DOWN)
    b_far = send(b_far, ACROSS)

    order = (1, 3, 0)
    given = line.step(*[columns(r, 1 - core) for r in order])
    got = [send(value, SWAP) for value in given]
    got = line.step(*got)
    for r, value in zip(order, got):
        features[r] = jnp.concatenate([columns(r, core), value], axis=0)
    b_rest = line.step(jnp.stack([term_b(r, 1).astype(BF) for r in order]))
    b_rest = send(b_rest, ACROSS)
    anchor_rows, local_rows = line.step(frag_anchor, frag_local[0])
    z_part = lax.psum_scatter(
        anchor_rows - local_rows,
        "island",
        scatter_dimension=0,
        axis_index_groups=Z_GROUPS,
        tiled=True,
    )

    a_low, a_high = line.step(a_low, a_high)
    a_up, a_down = term_a(1), term_a(3)
    a_up = jnp.concatenate([a_up[:, :half] + a_low.astype(F32), a_up[:, half:]], axis=1).astype(BF)
    a_down = jnp.concatenate(
        [a_down[:, :half], a_down[:, half:] + a_high.astype(F32)], axis=1
    ).astype(BF)
    a_up, a_down = line.step(a_up, a_down)
    a_from_down, a_from_up = send(a_up, UP), send(a_down, DOWN)

    b_far = line.step(b_far)
    b_far = line.step((term_b(2, 0) + b_far.astype(F32)).astype(BF))
    b_low, b_high = send(b_far[:half], UP), send(b_far[half:], DOWN)

    a_from_down, a_from_up = line.step(a_from_down, a_from_up)
    a_sum = term_a(0) + a_from_down.astype(F32) + a_from_up.astype(F32)
    a_here, a_sent = line.step(a_sum[0], a_sum[1].astype(BF))
    a_across = send(a_sent, ACROSS)

    b_rest, b_low, b_high = line.step(b_rest, b_low, b_high)
    b_up = term_b(1, 0) + b_rest[0].astype(F32)
    b_down = term_b(3, 0) + b_rest[1].astype(F32)
    b_here = term_b(0, 0) + b_rest[2].astype(F32)
    b_up = jnp.concatenate([b_up[:half] + b_low.astype(F32), b_up[half:]]).astype(BF)
    b_down = jnp.concatenate([b_down[:half], b_down[half:] + b_high.astype(F32)]).astype(BF)
    b_up, b_down = line.step(b_up, b_down)
    b_from_down, b_from_up = send(b_up, UP), send(b_down, DOWN)

    def inner_update(grad, part):
        master = key_master[0][:, part]
        first_new = BETA_ONE * key_first[0][:, part] + (1.0 - BETA_ONE) * grad
        second_new = BETA_TWO * key_second[0][:, part] + (1.0 - BETA_TWO) * grad * grad
        update = first_new / (jnp.sqrt(second_new) + EPSILON)
        master_new = master - INNER_RATE * (update + DECAY_RATE * master)
        return master_new, first_new, second_new

    z_part = line.step(z_part)
    z_other = lax.ppermute(z_part, "island", X_LO)

    a_across = line.step(a_across)
    a_state = inner_update(a_here + a_across.astype(F32), slice(0, SPLIT))
    a_own = line.step(a_state[0].astype(BF))
    a_other = send(a_own, ACROSS)

    b_from_down, b_from_up = line.step(b_from_down, b_from_up)
    b_state = inner_update(
        b_here + b_from_down.astype(F32) + b_from_up.astype(F32), slice(SPLIT, None)
    )
    b_own = line.step(b_state[0].astype(BF))
    b_of_down, b_of_up = send(b_own, UP), send(b_own, DOWN)
    b_own_x = send(b_own, ACROSS)

    z_other = line.step(z_other)
    share = line.step((z_part + z_other) / lax.axis_size("island"))
    outer_grad = lax.all_gather(share, "island", axis=0, axis_index_groups=Z_GROUPS, tiled=True)

    a_other = line.step(a_other)
    a_pair = line.step(jnp.stack([a_own, a_other]))
    a_of_down, a_of_up = send(a_pair, UP), send(a_pair, DOWN)

    b_of_down, b_of_up = line.step(b_of_down, b_of_up)
    b_near = jnp.stack([b_of_up, b_of_down])
    b_mid_low, b_mid_high, b_near = line.step(b_of_down[:half], b_of_up[half:], b_near)
    b_far_low, b_far_high = send(b_mid_low, UP), send(b_mid_high, DOWN)
    b_near_x = send(b_near, ACROSS)

    b_far_low, b_far_high = line.step(b_far_low, b_far_high)
    b_far_own = line.step(jnp.concatenate([b_far_low, b_far_high]))
    b_far_x = send(b_far_own, ACROSS)

    def product(r, block):
        return jnp.dot(features[r], block.reshape(2 * rows, -1), preferred_element_type=F32)

    join = lambda a, b: jnp.concatenate([a, b], axis=1)[None]
    a_keys = line.step(product(0, a_pair))
    states = line.step(*[join(a, b) for a, b in zip(a_state, b_state)])
    outer_grad = line.step(outer_grad)
    outer_state = line.step(*outer_update(outer_grad, frag_anchor, frag_momentum))

    a_of_down, a_of_up = line.step(a_of_down, a_of_up)
    a_mid_low, a_mid_high = line.step(a_of_down[:, :half], a_of_up[:, half:])
    a_far_low, a_far_high = send(a_mid_low, UP), send(a_mid_high, DOWN)
    a_keys = line.step(a_keys + product(1, a_of_up) + product(3, a_of_down))

    b_own_x = line.step(b_own_x)
    b_keys = line.step(product(0, jnp.stack([b_own, b_own_x])))
    b_near_x = line.step(b_near_x)
    b_keys += product(1, jnp.stack([b_near[0], b_near_x[0]]))
    b_keys += product(3, jnp.stack([b_near[1], b_near_x[1]]))
    b_keys = line.step(b_keys)
    a_far_low, a_far_high = line.step(a_far_low, a_far_high)
    a_keys = line.step(a_keys + product(2, jnp.concatenate([a_far_low, a_far_high], axis=1)))
    a_part = send(a_keys[count:], SWAP)
    b_far_x = line.step(b_far_x)
    b_keys = line.step(b_keys + product(2, jnp.stack([b_far_own, b_far_x])))
    b_part = send(b_keys[count:], SWAP)
    keys = join(a_keys[:count] + a_part, b_keys[:count] + b_part)
    return (*states, keys, *outer_state)


def solution(mesh):
    wide = P("island", "fsdp", None)
    flat = P("fsdp", None)
    return jax.shard_map(
        per_device,
        mesh=mesh,
        in_specs=(wide, wide, wide, wide, wide, wide, flat, flat),
        out_specs=(wide, wide, wide, wide, flat, flat),
        check_vma=False,
    )
```

```python
import functools

import jax
import jax.numpy as jnp
from jax import lax
from jax.experimental import pallas as pl
from jax.experimental.pallas import tpu as pltpu
from jax.sharding import PartitionSpec as P

BETA_ONE = 0.9
BETA_TWO = 0.95
INNER_RATE = 0.002
DECAY_RATE = 0.1
EPSILON = 1e-08
OUTER_RATE = 0.7
OUTER_MOMENT = 0.9

BF = jnp.bfloat16
F32 = jnp.float32

N_Y = 4
N_FSDP = 16
N_ISLAND = 8
CHEAP = pl.CostEstimate(flops=1, bytes_accessed=1, transcendentals=0)


def place(x_hi, y, core):
    return (x_hi % 2) * 8 + (y % N_Y) * 2 + core % 2


def moves(d_x, d_y, d_core):
    pairs = []
    for index in range(N_FSDP):
        x_hi, y, core = index // 8, (index // 2) % N_Y, index % 2
        pairs.append((index, place(x_hi + d_x, y + d_y, core + d_core)))
    return pairs


SPLIT = 640

SWAP = moves(0, 0, 1)
ACROSS = moves(1, 0, 0)
UP = moves(0, 1, 0)
DOWN = moves(0, -1, 0)


Z_GROUPS = [[2 * z + x_lo for z in range(4)] for x_lo in range(2)]
X_LO = [(i, i ^ 1) for i in range(N_ISLAND)]


def send(value, pairs):
    return lax.ppermute(value, "fsdp", pairs)


class Line:
    def __init__(self):
        self.mark = ()

    def step(self, *values):
        out = lax.optimization_barrier((*values, *self.mark))[: len(values)]
        self.mark = tuple(out)
        return out[0] if len(values) == 1 else out

    def hold(self, *values):
        out = lax.optimization_barrier((*values, *self.mark))[: len(values)]
        return out[0] if len(values) == 1 else out


def shape(dims, dtype):
    return jax.ShapeDtypeStruct(dims, dtype)


def kernel_call(body, where, operands, grid, in_specs, out_specs, out_shape, scratch=(), alias=None, room=20):
    return pl.pallas_call(
        body,
        out_shape=out_shape,
        grid_spec=pltpu.PrefetchScalarGridSpec(
            num_scalar_prefetch=1,
            grid=grid,
            in_specs=in_specs,
            out_specs=out_specs,
            scratch_shapes=list(scratch),
        ),
        input_output_aliases=alias or {},
        compiler_params=pltpu.CompilerParams(vmem_limit_bytes=room * 1024 * 1024),
        cost_estimate=CHEAP,
    )(where, *operands)


def split_body(where, theirs, mine, sent, kept):
    sent[...] = theirs[...]
    kept[...] = mine[...]


def split_columns(tokens, where, rows):
    count = tokens.shape[0]
    steps = where.shape[0] // 2
    block = pl.BlockSpec((count, rows), lambda i, where: (0, i))
    return kernel_call(
        split_body,
        where,
        (tokens, tokens),
        (steps,),
        [
            pl.BlockSpec((count, rows), lambda i, where: (0, where[i])),
            pl.BlockSpec((count, rows), lambda i, where: (0, where[steps + i])),
        ],
        [block, block],
        [
            shape((count, steps * rows), tokens.dtype),
            shape((2 * count, steps * rows), tokens.dtype),
        ],
        room=8,
    )


def fill_body(where, source, old, out):
    out[...] = source[...]


def fill_lower(source, old):
    count, width = source.shape
    size = width // 3
    return kernel_call(
        fill_body,
        jnp.zeros((1,), jnp.int32),
        (source, old),
        (3,),
        [
            pl.BlockSpec((count, size), lambda i, where: (0, i)),
            pl.BlockSpec(memory_space=pl.ANY),
        ],
        pl.BlockSpec((count, size), lambda i, where: (1, i)),
        shape(old.shape, old.dtype),
        alias={2: 0},
        room=8,
    )


def keys_body(joined, where, *refs):
    number = len(joined)
    lhs, refs, out = refs[:number], list(refs[number:-1]), refs[-1]
    weights = []
    for whole in joined:
        first = refs.pop(0)
        weights.append((first, first) if whole else (first, refs.pop(0)))
    for k, part in enumerate((slice(0, SPLIT), slice(SPLIT, None))):
        total = refs[0][:, part] if refs else None
        for features, pair, whole in zip(lhs, weights, joined):
            weight = pair[k][:, part] if whole else pair[k][...]
            value = jnp.dot(features[...], weight, preferred_element_type=F32)
            total = value if total is None else total + value
        out[:, part] = total


def keys_call(rows, first, count, terms, before=None):
    tile = min(256, count)
    skip = first // tile
    size = key_width(terms[0][1])
    operands, specs = [], []
    for (array, at), _ in terms:
        operands.append(array)
        specs.append(pl.BlockSpec((tile, rows), functools.partial(lambda at, i, where: (i + skip, at), at)))
    for _, parts in terms:
        for part in parts:
            operands.append(part)
            specs.append(pl.BlockSpec(part.shape, lambda i, where: (0, 0)))
    if before is not None:
        operands.append(before)
        specs.append(pl.BlockSpec((tile, size), lambda i, where: (i + skip, 0)))
    return kernel_call(
        functools.partial(keys_body, [len(parts) == 1 for _, parts in terms]),
        jnp.zeros((1,), jnp.int32),
        operands,
        (count // tile,),
        specs,
        pl.BlockSpec((tile, size), lambda i, where: (i, 0)),
        shape((count, size), F32),
    )


def key_width(parts):
    return sum(part.shape[1] for part in parts)


def pieces_body(where, near_up, near_dn, across, other, near, low, high):
    count, half = near_up.shape[0], near_up.shape[0] // 2
    other[...] = across[:, :SPLIT]
    near[:count] = near_up[:, SPLIT:]
    near[count:] = near_dn[:, SPLIT:]
    low[...] = near_dn[:half]
    high[...] = near_up[half:]


def gather_pieces(near_up, near_dn, across):
    rows, width = across.shape
    outs = [
        (rows, SPLIT),
        (2 * rows, width - SPLIT),
        (rows // 2, width),
        (rows // 2, width),
    ]
    full = lambda dims: pl.BlockSpec(dims, lambda i, where: (0, 0))
    return kernel_call(
        pieces_body,
        jnp.zeros((1,), jnp.int32),
        (near_up, near_dn, across),
        (1,),
        [full((rows, width))] * 3,
        [full(dims) for dims in outs],
        [shape(dims, across.dtype) for dims in outs],
        room=16,
    )


def wide(value):
    return value.astype(F32)


def per_device(
    tokens, key_grad_out, key_master, key_first, key_second, frag_local, frag_anchor, frag_momentum
):
    me = lax.axis_index("fsdp")
    x_hi, y, core = me // 8, (me // 2) % N_Y, me % 2
    tok = tokens[0]
    up = key_grad_out[0]
    count, width = tok.shape
    rows = width // N_FSDP
    half = rows // 2
    line = Line()

    def spots(which_core, *blocks):
        return jnp.stack([place(x_hi + p, y + r, which_core) for r, p in blocks]).astype(jnp.int32)

    def far_columns(source, which_core):
        return jnp.concatenate(
            [
                lax.dynamic_slice(
                    source, (0, place(x_hi + p, y + 2, which_core) * rows), (count, rows)
                )
                for p in range(2)
            ],
            axis=1,
        )

    rest_blocks = ((1, 0), (1, 1), (0, 1), (3, 1), (3, 0), (0, 0))

    other_up = send(up, SWAP)
    far_sent = line.step(far_columns(tok, 1 - core))
    got_far = send(far_sent, SWAP)
    share = lax.psum_scatter(
        line.step(frag_anchor - frag_local[0]),
        "island",
        scatter_dimension=0,
        axis_index_groups=Z_GROUPS,
        tiled=True,
    )
    other_up, got_far = line.step(other_up, got_far)
    up_all = jnp.concatenate([up, other_up], axis=0)
    far_all = jnp.concatenate([far_columns(tok, core), got_far], axis=0)
    up_a, up_b = up_all[:, :SPLIT], up_all[:, SPLIT:]

    def transposed(lhs, upstream):
        return lax.dot_general(
            lhs, upstream, (((0,), (0,)), ((), ())), preferred_element_type=F32
        )

    def rest_term(first, number, upstream):
        return transposed(rest_all[:, first * rows : (first + number) * rows], upstream)

    a_far1, a_far0, b_far = line.step(
        transposed(far_all[:, rows:], up_a).astype(BF),
        transposed(far_all[:, :rows], up_a).astype(BF),
        transposed(far_all[:, rows:], up_b).astype(BF),
    )
    a_far1 = send(a_far1, DOWN)
    a_far0 = send(a_far0, UP)
    b_far = send(b_far, ACROSS)

    where = jnp.concatenate([spots(1 - core, *rest_blocks), spots(core, *rest_blocks)])
    rest_sent, rest_kept = line.step(*split_columns(line.hold(tok), where, rows))
    got_rest = send(rest_sent, SWAP)
    got_rest = line.step(got_rest)
    rest_all = line.step(fill_lower(got_rest, rest_kept))
    b_rest = line.step(rest_term(1, 3, up_b).astype(BF))
    b_rest = send(b_rest, ACROSS)
    a_one, a_three = line.step(rest_term(0, 2, up_a), rest_term(3, 2, up_a))
    b_two = line.step(transposed(far_all[:, :rows], up_b))
    share = line.step(share)
    share_other = lax.ppermute(share, "island", X_LO)

    a_far0, a_far1, b_far = line.step(a_far0, a_far1, b_far)
    up_sent = jnp.concatenate([a_one[:rows] + wide(a_far0), a_one[rows:]]).astype(BF)
    down_sent = jnp.concatenate([a_three[:rows] + wide(a_far1), a_three[rows:]]).astype(BF)
    b_low, b_high = (
        (b_two[:half] + wide(b_far[:half])).astype(BF),
        (b_two[half:] + wide(b_far[half:])).astype(BF),
    )
    up_sent, down_sent, b_low, b_high = line.step(up_sent, down_sent, b_low, b_high)
    from_down, from_up = send(up_sent, UP), send(down_sent, DOWN)
    b_low, b_high = send(b_low, UP), send(b_high, DOWN)

    from_down, from_up, rest_all, share_other = line.step(from_down, from_up, rest_all, share_other)
    a_side = rest_term(2, 1, up_a) + wide(from_down[rows:]) + wide(from_up[:rows])
    a_side = line.step(a_side.astype(BF))
    a_side = send(a_side, ACROSS)
    share, rest_all = line.step(share + share_other, rest_all)
    total = lax.all_gather(share, "island", axis=0, axis_index_groups=Z_GROUPS, tiled=True)
    from_down, from_up = line.hold(from_down, from_up)
    a_here = rest_term(5, 1, up_a) + wide(from_down[:rows]) + wide(from_up[rows:])
    a_here = line.step(a_here)
    b_one, b_three = line.step(rest_term(0, 1, up_b), rest_term(4, 2, up_b))

    b_rest, b_low, b_high = line.step(b_rest, b_low, b_high)
    b_up = b_one + wide(b_rest[:rows])
    b_here = b_three[rows:] + wide(b_rest[rows : 2 * rows])
    b_down = b_three[:rows] + wide(b_rest[2 * rows :])
    b_up = jnp.concatenate([b_up[:half] + wide(b_low), b_up[half:]]).astype(BF)
    b_down = jnp.concatenate([b_down[:half], b_down[half:] + wide(b_high)]).astype(BF)
    b_up, b_down, b_here = line.step(b_up, b_down, b_here)
    b_up, b_down = send(b_up, UP), send(b_down, DOWN)

    def inner_update(grad, part):
        master = key_master[0][:, part]
        first_new = BETA_ONE * key_first[0][:, part] + (1.0 - BETA_ONE) * grad
        second_new = BETA_TWO * key_second[0][:, part] + (1.0 - BETA_TWO) * grad * grad
        update = first_new / (jnp.sqrt(second_new) + EPSILON)
        master_new = master - INNER_RATE * (update + DECAY_RATE * master)
        return master_new, first_new, second_new

    a_side, b_up, b_down = line.step(a_side, b_up, b_down)
    grad = jnp.concatenate(
        [a_here + wide(a_side), b_here + wide(b_up) + wide(b_down)], axis=1
    )
    w, grad = line.step(inner_update(grad, slice(None))[0].astype(BF), grad)
    w_dn, w_up, w_x = send(w, UP), send(w, DOWN), send(w, ACROSS)
    states = line.step(*inner_update(grad, slice(None)))
    total, momentum_rows = line.step(total, frag_momentum)
    outer_grad = total / N_ISLAND
    new_momentum = OUTER_MOMENT * momentum_rows + outer_grad
    new_anchor = frag_anchor - OUTER_RATE * (outer_grad + OUTER_MOMENT * new_momentum)
    new_anchor, new_momentum = line.step(new_anchor, new_momentum)

    w_dn, w_up, w_x = line.step(w_dn, w_up, w_x)
    other, near, low, high = line.step(*gather_pieces(w_up, w_dn, w_x))
    near_x = send(near, ACROSS)
    low, high = send(low, UP), send(high, DOWN)
    o_dn, o_up = send(other, UP), send(other, DOWN)
    at = rest_blocks.index
    rest_late = line.hold(rest_all)
    keys = line.step(
        keys_call(
            rows,
            0,
            2 * count,
            [
                ((rest_late, at(b)), (v,))
                for b, v in (((1, 0), w_up), ((3, 0), w_dn), ((0, 0), w), ((0, 1), w_x))
            ],
        )
    )

    near_x, low, high, o_dn, o_up = line.step(near_x, low, high, o_dn, o_up)
    far_low, far_high = low, high
    far_b = jnp.concatenate([low[:, SPLIT:], high[:, SPLIT:]])
    far_b, low, high = line.step(far_b, o_dn[:half], o_up[half:])
    far_x = send(far_b, ACROSS)
    low, high = send(low, UP), send(high, DOWN)
    rest_late, far_low, far_high = line.hold(rest_all, far_low, far_high)
    w_far = jnp.concatenate([far_low, far_high])
    keys = line.step(
        keys_call(
            rows,
            0,
            2 * count,
            [
                ((rest_late, at((1, 1))), (o_up, near_x[:rows])),
                ((rest_late, at((3, 1))), (o_dn, near_x[rows:])),
                ((far_all, 0), (w_far,)),
            ],
            keys,
        )
    )
    far_x, low, high = line.step(far_x, low, high)
    last = [((far_all, 1), (jnp.concatenate([low, high]), far_x))]
    part = line.step(keys_call(rows, count, count, last, keys))
    part = send(part, SWAP)
    mine = keys_call(rows, 0, count, last, keys)
    return (*(v[None] for v in states), (mine + part)[None], new_anchor, new_momentum)


def solution(mesh):
    whole = P("island", "fsdp", None)
    flat = P("fsdp", None)
    return jax.shard_map(
        per_device,
        mesh=mesh,
        in_specs=(whole,) * 6 + (flat, flat),
        out_specs=(whole,) * 4 + (flat, flat),
        check_vma=False,
    )
```

```python
import functools

import jax
import jax.numpy as jnp
from jax import lax
from jax.experimental import pallas as pl
from jax.experimental.pallas import tpu as pltpu
from jax.sharding import PartitionSpec as P

BETA_ONE = 0.9
BETA_TWO = 0.95
INNER_RATE = 0.002
DECAY_RATE = 0.1
EPSILON = 1e-08
OUTER_RATE = 0.7
OUTER_MOMENT = 0.9

BF = jnp.bfloat16
F32 = jnp.float32

N_Y = 4
N_FSDP = 16
N_ISLAND = 8
CHEAP = pl.CostEstimate(flops=1, bytes_accessed=1, transcendentals=0)


def place(x_hi, y, core):
    return (x_hi % 2) * 8 + (y % N_Y) * 2 + core % 2


def moves(d_x, d_y, d_core):
    pairs = []
    for index in range(N_FSDP):
        x_hi, y, core = index // 8, (index // 2) % N_Y, index % 2
        pairs.append((index, place(x_hi + d_x, y + d_y, core + d_core)))
    return pairs


SPLIT = 640

SWAP = moves(0, 0, 1)
ACROSS = moves(1, 0, 0)
UP = moves(0, 1, 0)
DOWN = moves(0, -1, 0)


Z_GROUPS = [[2 * z + x_lo for z in range(4)] for x_lo in range(2)]
X_LO = [(i, i ^ 1) for i in range(N_ISLAND)]


def send(value, pairs):
    return lax.ppermute(value, "fsdp", pairs)


class Line:
    def __init__(self):
        self.mark = ()

    def step(self, *values):
        out = lax.optimization_barrier((*values, *self.mark))[: len(values)]
        self.mark = tuple(out)
        return out[0] if len(values) == 1 else out

    def hold(self, *values):
        out = lax.optimization_barrier((*values, *self.mark))[: len(values)]
        return out[0] if len(values) == 1 else out


def shape(dims, dtype):
    return jax.ShapeDtypeStruct(dims, dtype)


def kernel_call(body, where, operands, grid, in_specs, out_specs, out_shape, scratch=(), alias=None, room=20):
    return pl.pallas_call(
        body,
        out_shape=out_shape,
        grid_spec=pltpu.PrefetchScalarGridSpec(
            num_scalar_prefetch=1,
            grid=grid,
            in_specs=in_specs,
            out_specs=out_specs,
            scratch_shapes=list(scratch),
        ),
        input_output_aliases=alias or {},
        compiler_params=pltpu.CompilerParams(vmem_limit_bytes=room * 1024 * 1024),
        cost_estimate=CHEAP,
    )(where, *operands)


def split_body(where, theirs, mine, sent, kept):
    sent[...] = theirs[...]
    kept[...] = mine[...]


def split_columns(tokens, where, rows):
    count = tokens.shape[0]
    steps = where.shape[0] // 2
    block = pl.BlockSpec((count, rows), lambda i, where: (0, i))
    return kernel_call(
        split_body,
        where,
        (tokens, tokens),
        (steps,),
        [
            pl.BlockSpec((count, rows), lambda i, where: (0, where[i])),
            pl.BlockSpec((count, rows), lambda i, where: (0, where[steps + i])),
        ],
        [block, block],
        [
            shape((count, steps * rows), tokens.dtype),
            shape((2 * count, steps * rows), tokens.dtype),
        ],
        room=8,
    )


def fill_body(where, source, old, out):
    out[...] = source[...]


def fill_lower(source, old):
    count, width = source.shape
    size = width // 3
    return kernel_call(
        fill_body,
        jnp.zeros((1,), jnp.int32),
        (source, old),
        (3,),
        [
            pl.BlockSpec((count, size), lambda i, where: (0, i)),
            pl.BlockSpec(memory_space=pl.ANY),
        ],
        pl.BlockSpec((count, size), lambda i, where: (1, i)),
        shape(old.shape, old.dtype),
        alias={2: 0},
        room=8,
    )


def keys_body(joined, where, *refs):
    number = len(joined)
    lhs, refs, out = refs[:number], list(refs[number:-1]), refs[-1]
    weights = []
    for whole in joined:
        first = refs.pop(0)
        weights.append((first, first) if whole else (first, refs.pop(0)))
    for k, part in enumerate((slice(0, SPLIT), slice(SPLIT, None))):
        total = refs[0][:, part] if refs else None
        for features, pair, whole in zip(lhs, weights, joined):
            weight = pair[k][:, part] if whole else pair[k][...]
            value = jnp.dot(features[...], weight, preferred_element_type=F32)
            total = value if total is None else total + value
        out[:, part] = total


def keys_call(rows, first, count, terms, before=None):
    tile = min(256, count)
    skip = first // tile
    size = key_width(terms[0][1])
    operands, specs = [], []
    for (array, at), _ in terms:
        operands.append(array)
        specs.append(pl.BlockSpec((tile, rows), functools.partial(lambda at, i, where: (i + skip, at), at)))
    for _, parts in terms:
        for part in parts:
            operands.append(part)
            specs.append(pl.BlockSpec(part.shape, lambda i, where: (0, 0)))
    if before is not None:
        operands.append(before)
        specs.append(pl.BlockSpec((tile, size), lambda i, where: (i + skip, 0)))
    return kernel_call(
        functools.partial(keys_body, [len(parts) == 1 for _, parts in terms]),
        jnp.zeros((1,), jnp.int32),
        operands,
        (count // tile,),
        specs,
        pl.BlockSpec((tile, size), lambda i, where: (i, 0)),
        shape((count, size), F32),
    )


def key_width(parts):
    return sum(part.shape[1] for part in parts)


def pieces_body(where, near_up, near_dn, across, other, near, low, high):
    count, half = near_up.shape[0], near_up.shape[0] // 2
    other[...] = across[:, :SPLIT]
    near[:count] = near_up[:, SPLIT:]
    near[count:] = near_dn[:, SPLIT:]
    low[...] = near_dn[:half]
    high[...] = near_up[half:]


def gather_pieces(near_up, near_dn, across):
    rows, width = across.shape
    outs = [
        (rows, SPLIT),
        (2 * rows, width - SPLIT),
        (rows // 2, width),
        (rows // 2, width),
    ]
    full = lambda dims: pl.BlockSpec(dims, lambda i, where: (0, 0))
    return kernel_call(
        pieces_body,
        jnp.zeros((1,), jnp.int32),
        (near_up, near_dn, across),
        (1,),
        [full((rows, width))] * 3,
        [full(dims) for dims in outs],
        [shape(dims, across.dtype) for dims in outs],
        room=16,
    )


def wide(value):
    return value.astype(F32)


def per_device(
    tokens, key_grad_out, key_master, key_first, key_second, frag_local, frag_anchor, frag_momentum
):
    me = lax.axis_index("fsdp")
    x_hi, y, core = me // 8, (me // 2) % N_Y, me % 2
    tok = tokens[0]
    up = key_grad_out[0]
    count, width = tok.shape
    rows = width // N_FSDP
    half = rows // 2
    line = Line()

    def spots(which_core, *blocks):
        return jnp.stack([place(x_hi + p, y + r, which_core) for r, p in blocks]).astype(jnp.int32)

    def far_columns(source, which_core):
        return jnp.concatenate(
            [
                lax.dynamic_slice(
                    source, (0, place(x_hi + p, y + 2, which_core) * rows), (count, rows)
                )
                for p in range(2)
            ],
            axis=1,
        )

    rest_blocks = ((1, 0), (1, 1), (0, 1), (3, 1), (3, 0), (0, 0))

    other_up = send(up, SWAP)
    far_sent = line.step(far_columns(tok, 1 - core))
    got_far = send(far_sent, SWAP)
    share = lax.psum_scatter(
        line.step(frag_anchor - frag_local[0]),
        "island",
        scatter_dimension=0,
        axis_index_groups=Z_GROUPS,
        tiled=True,
    )
    other_up, got_far = line.step(other_up, got_far)
    up_all = jnp.concatenate([up, other_up], axis=0)
    far_all = jnp.concatenate([far_columns(tok, core), got_far], axis=0)
    up_a, up_b = up_all[:, :SPLIT], up_all[:, SPLIT:]

    def transposed(lhs, upstream):
        return lax.dot_general(
            lhs, upstream, (((0,), (0,)), ((), ())), preferred_element_type=F32
        )

    def rest_term(first, number, upstream):
        return transposed(rest_all[:, first * rows : (first + number) * rows], upstream)

    a_far1, a_far0, b_far = line.step(
        transposed(far_all[:, rows:], up_a).astype(BF),
        transposed(far_all[:, :rows], up_a).astype(BF),
        transposed(far_all[:, rows:], up_b).astype(BF),
    )
    a_far1 = send(a_far1, DOWN)
    a_far0 = send(a_far0, UP)
    b_far = send(b_far, ACROSS)

    where = jnp.concatenate([spots(1 - core, *rest_blocks), spots(core, *rest_blocks)])
    rest_sent, rest_kept = line.step(*split_columns(line.hold(tok), where, rows))
    got_rest = send(rest_sent, SWAP)
    got_rest = line.step(got_rest)
    rest_all = line.step(fill_lower(got_rest, rest_kept))
    b_rest = line.step(rest_term(1, 3, up_b).astype(BF))
    b_rest = send(b_rest, ACROSS)
    a_one = line.step(rest_term(0, 2, up_a))
    share = line.step(share)
    share_other = lax.ppermute(share, "island", X_LO)
    a_three = line.step(rest_term(3, 2, up_a))
    b_two = line.step(transposed(far_all[:, :rows], up_b))

    a_far0, a_far1, b_far = line.step(a_far0, a_far1, b_far)
    up_sent = jnp.concatenate([a_one[:rows] + wide(a_far0), a_one[rows:]]).astype(BF)
    down_sent = jnp.concatenate([a_three[:rows] + wide(a_far1), a_three[rows:]]).astype(BF)
    b_low, b_high = (
        (b_two[:half] + wide(b_far[:half])).astype(BF),
        (b_two[half:] + wide(b_far[half:])).astype(BF),
    )
    up_sent, down_sent, b_low, b_high = line.step(up_sent, down_sent, b_low, b_high)
    from_down, from_up = send(up_sent, UP), send(down_sent, DOWN)
    b_low, b_high = send(b_low, UP), send(b_high, DOWN)

    from_down, from_up, rest_all, share_other = line.step(from_down, from_up, rest_all, share_other)
    a_side = rest_term(2, 1, up_a) + wide(from_down[rows:]) + wide(from_up[:rows])
    a_side = line.step(a_side.astype(BF))
    a_side = send(a_side, ACROSS)
    share, rest_all = line.step(share + share_other, rest_all)
    total = lax.all_gather(share, "island", axis=0, axis_index_groups=Z_GROUPS, tiled=True)
    from_down, from_up = line.hold(from_down, from_up)
    a_here = rest_term(5, 1, up_a) + wide(from_down[:rows]) + wide(from_up[rows:])
    a_here = line.step(a_here)
    b_one, b_three = line.step(rest_term(0, 1, up_b), rest_term(4, 2, up_b))

    b_rest, b_low, b_high = line.step(b_rest, b_low, b_high)
    b_up = b_one + wide(b_rest[:rows])
    b_here = b_three[rows:] + wide(b_rest[rows : 2 * rows])
    b_down = b_three[:rows] + wide(b_rest[2 * rows :])
    b_up = jnp.concatenate([b_up[:half] + wide(b_low), b_up[half:]]).astype(BF)
    b_down = jnp.concatenate([b_down[:half], b_down[half:] + wide(b_high)]).astype(BF)
    b_up, b_down, b_here = line.step(b_up, b_down, b_here)
    b_up, b_down = send(b_up, UP), send(b_down, DOWN)

    def inner_update(grad, part):
        master = key_master[0][:, part]
        first_new = BETA_ONE * key_first[0][:, part] + (1.0 - BETA_ONE) * grad
        second_new = BETA_TWO * key_second[0][:, part] + (1.0 - BETA_TWO) * grad * grad
        update = first_new / (jnp.sqrt(second_new) + EPSILON)
        master_new = master - INNER_RATE * (update + DECAY_RATE * master)
        return master_new, first_new, second_new

    a_side, b_up, b_down = line.step(a_side, b_up, b_down)
    grad = jnp.concatenate(
        [a_here + wide(a_side), b_here + wide(b_up) + wide(b_down)], axis=1
    )
    w, grad = line.step(inner_update(grad, slice(None))[0].astype(BF), grad)
    w_dn, w_up, w_x = send(w, UP), send(w, DOWN), send(w, ACROSS)
    states = line.step(*inner_update(grad, slice(None)))
    total, momentum_rows = line.step(total, frag_momentum)
    outer_grad = total / N_ISLAND
    new_momentum = OUTER_MOMENT * momentum_rows + outer_grad
    new_anchor = frag_anchor - OUTER_RATE * (outer_grad + OUTER_MOMENT * new_momentum)
    new_anchor, new_momentum = line.step(new_anchor, new_momentum)

    w_dn, w_up, w_x = line.step(w_dn, w_up, w_x)
    other, near, low, high = line.step(*gather_pieces(w_up, w_dn, w_x))
    near_x = send(near, ACROSS)
    low, high = send(low, UP), send(high, DOWN)
    o_dn, o_up = send(other, UP), send(other, DOWN)
    at = rest_blocks.index
    rest_late = line.hold(rest_all)
    keys = line.step(
        keys_call(
            rows,
            0,
            2 * count,
            [
                ((rest_late, at(b)), (v,))
                for b, v in (((1, 0), w_up), ((3, 0), w_dn), ((0, 0), w), ((0, 1), w_x))
            ],
        )
    )

    near_x, low, high, o_dn, o_up = line.step(near_x, low, high, o_dn, o_up)
    far_low, far_high = low, high
    far_b = jnp.concatenate([low[:, SPLIT:], high[:, SPLIT:]])
    far_b, low, high = line.step(far_b, o_dn[:half], o_up[half:])
    far_x = send(far_b, ACROSS)
    low, high = send(low, UP), send(high, DOWN)
    rest_late, far_low, far_high = line.hold(rest_all, far_low, far_high)
    w_far = jnp.concatenate([far_low, far_high])
    keys = line.step(
        keys_call(
            rows,
            0,
            2 * count,
            [
                ((rest_late, at((1, 1))), (o_up, near_x[:rows])),
                ((rest_late, at((3, 1))), (o_dn, near_x[rows:])),
                ((far_all, 0), (w_far,)),
            ],
            keys,
        )
    )
    far_x, low, high = line.step(far_x, low, high)
    last = [((far_all, 1), (jnp.concatenate([low, high]), far_x))]
    part = line.step(keys_call(rows, count, count, last, keys))
    part = send(part, SWAP)
    mine = keys_call(rows, 0, count, last, keys)
    return (*(v[None] for v in states), (mine + part)[None], new_anchor, new_momentum)


def solution(mesh):
    whole = P("island", "fsdp", None)
    flat = P("fsdp", None)
    return jax.shard_map(
        per_device,
        mesh=mesh,
        in_specs=(whole,) * 6 + (flat, flat),
        out_specs=(whole,) * 4 + (flat, flat),
        check_vma=False,
    )
```

```python
import functools

import jax
import jax.numpy as jnp
from jax import lax
from jax.experimental import pallas as pl
from jax.experimental.pallas import tpu as pltpu
from jax.sharding import PartitionSpec as P

BETA_ONE = 0.9
BETA_TWO = 0.95
INNER_RATE = 0.002
DECAY_RATE = 0.1
EPSILON = 1e-08
OUTER_RATE = 0.7
OUTER_MOMENT = 0.9

BF = jnp.bfloat16
F32 = jnp.float32

N_Y = 4
N_FSDP = 16
N_ISLAND = 8
CHEAP = pl.CostEstimate(flops=1, bytes_accessed=1, transcendentals=0)


def place(x_hi, y, core):
    return (x_hi % 2) * 8 + (y % N_Y) * 2 + core % 2


def moves(d_x, d_y, d_core):
    pairs = []
    for index in range(N_FSDP):
        x_hi, y, core = index // 8, (index // 2) % N_Y, index % 2
        pairs.append((index, place(x_hi + d_x, y + d_y, core + d_core)))
    return pairs


SPLIT = 640

SWAP = moves(0, 0, 1)
ACROSS = moves(1, 0, 0)
UP = moves(0, 1, 0)
DOWN = moves(0, -1, 0)


Z_GROUPS = [[2 * z + x_lo for z in range(4)] for x_lo in range(2)]
X_LO = [(i, i ^ 1) for i in range(N_ISLAND)]


def send(value, pairs):
    return lax.ppermute(value, "fsdp", pairs)


class Line:
    def __init__(self):
        self.mark = ()

    def step(self, *values):
        out = lax.optimization_barrier((*values, *self.mark))[: len(values)]
        self.mark = tuple(out)
        return out[0] if len(values) == 1 else out

    def hold(self, *values):
        out = lax.optimization_barrier((*values, *self.mark))[: len(values)]
        return out[0] if len(values) == 1 else out


def shape(dims, dtype):
    return jax.ShapeDtypeStruct(dims, dtype)


def kernel_call(body, where, operands, grid, in_specs, out_specs, out_shape, scratch=(), alias=None, room=20):
    return pl.pallas_call(
        body,
        out_shape=out_shape,
        grid_spec=pltpu.PrefetchScalarGridSpec(
            num_scalar_prefetch=1,
            grid=grid,
            in_specs=in_specs,
            out_specs=out_specs,
            scratch_shapes=list(scratch),
        ),
        input_output_aliases=alias or {},
        compiler_params=pltpu.CompilerParams(vmem_limit_bytes=room * 1024 * 1024),
        cost_estimate=CHEAP,
    )(where, *operands)


def split_body(where, theirs, mine, sent, kept):
    sent[...] = theirs[...]
    kept[...] = mine[...]


def split_columns(tokens, where, rows):
    count = tokens.shape[0]
    steps = where.shape[0] // 2
    block = pl.BlockSpec((count, rows), lambda i, where: (0, i))
    return kernel_call(
        split_body,
        where,
        (tokens, tokens),
        (steps,),
        [
            pl.BlockSpec((count, rows), lambda i, where: (0, where[i])),
            pl.BlockSpec((count, rows), lambda i, where: (0, where[steps + i])),
        ],
        [block, block],
        [
            shape((count, steps * rows), tokens.dtype),
            shape((2 * count, steps * rows), tokens.dtype),
        ],
        room=8,
    )


def fill_body(where, source, old, out):
    out[...] = source[...]


def fill_lower(source, old):
    count, width = source.shape
    size = width // 3
    return kernel_call(
        fill_body,
        jnp.zeros((1,), jnp.int32),
        (source, old),
        (3,),
        [
            pl.BlockSpec((count, size), lambda i, where: (0, i)),
            pl.BlockSpec(memory_space=pl.ANY),
        ],
        pl.BlockSpec((count, size), lambda i, where: (1, i)),
        shape(old.shape, old.dtype),
        alias={2: 0},
        room=8,
    )


def keys_body(joined, where, *refs):
    number = len(joined)
    lhs, refs, out = refs[:number], list(refs[number:-1]), refs[-1]
    weights = []
    for whole in joined:
        first = refs.pop(0)
        weights.append((first, first) if whole else (first, refs.pop(0)))
    for k, part in enumerate((slice(0, SPLIT), slice(SPLIT, None))):
        total = refs[0][:, part] if refs else None
        for features, pair, whole in zip(lhs, weights, joined):
            weight = pair[k][:, part] if whole else pair[k][...]
            value = jnp.dot(features[...], weight, preferred_element_type=F32)
            total = value if total is None else total + value
        out[:, part] = total


def keys_call(rows, first, count, terms, before=None):
    tile = min(256, count)
    skip = first // tile
    size = key_width(terms[0][1])
    operands, specs = [], []
    for (array, at), _ in terms:
        operands.append(array)
        specs.append(pl.BlockSpec((tile, rows), functools.partial(lambda at, i, where: (i + skip, at), at)))
    for _, parts in terms:
        for part in parts:
            operands.append(part)
            specs.append(pl.BlockSpec(part.shape, lambda i, where: (0, 0)))
    if before is not None:
        operands.append(before)
        specs.append(pl.BlockSpec((tile, size), lambda i, where: (i + skip, 0)))
    return kernel_call(
        functools.partial(keys_body, [len(parts) == 1 for _, parts in terms]),
        jnp.zeros((1,), jnp.int32),
        operands,
        (count // tile,),
        specs,
        pl.BlockSpec((tile, size), lambda i, where: (i, 0)),
        shape((count, size), F32),
    )


def key_width(parts):
    return sum(part.shape[1] for part in parts)


def pieces_body(where, near_up, near_dn, across, other, near, low, high):
    count, half = near_up.shape[0], near_up.shape[0] // 2
    other[...] = across[:, :SPLIT]
    near[:count] = near_up[:, SPLIT:]
    near[count:] = near_dn[:, SPLIT:]
    low[...] = near_dn[:half]
    high[...] = near_up[half:]


def gather_pieces(near_up, near_dn, across):
    rows, width = across.shape
    outs = [
        (rows, SPLIT),
        (2 * rows, width - SPLIT),
        (rows // 2, width),
        (rows // 2, width),
    ]
    full = lambda dims: pl.BlockSpec(dims, lambda i, where: (0, 0))
    return kernel_call(
        pieces_body,
        jnp.zeros((1,), jnp.int32),
        (near_up, near_dn, across),
        (1,),
        [full((rows, width))] * 3,
        [full(dims) for dims in outs],
        [shape(dims, across.dtype) for dims in outs],
        room=16,
    )


def wide(value):
    return value.astype(F32)


def per_device(
    tokens, key_grad_out, key_master, key_first, key_second, frag_local, frag_anchor, frag_momentum
):
    me = lax.axis_index("fsdp")
    x_hi, y, core = me // 8, (me // 2) % N_Y, me % 2
    tok = tokens[0]
    up = key_grad_out[0]
    count, width = tok.shape
    rows = width // N_FSDP
    half = rows // 2
    line = Line()

    def spots(which_core, *blocks):
        return jnp.stack([place(x_hi + p, y + r, which_core) for r, p in blocks]).astype(jnp.int32)

    def far_columns(source, which_core):
        return jnp.concatenate(
            [
                lax.dynamic_slice(
                    source, (0, place(x_hi + p, y + 2, which_core) * rows), (count, rows)
                )
                for p in range(2)
            ],
            axis=1,
        )

    rest_blocks = ((1, 0), (1, 1), (0, 1), (3, 1), (3, 0), (0, 0))

    other_up = send(up, SWAP)
    far_sent = line.step(far_columns(tok, 1 - core))
    got_far = send(far_sent, SWAP)
    share = lax.psum_scatter(
        line.step(frag_anchor - frag_local[0]),
        "island",
        scatter_dimension=0,
        axis_index_groups=Z_GROUPS,
        tiled=True,
    )
    other_up, got_far = line.step(other_up, got_far)
    up_all = jnp.concatenate([up, other_up], axis=0)
    far_all = jnp.concatenate([far_columns(tok, core), got_far], axis=0)
    up_a, up_b = up_all[:, :SPLIT], up_all[:, SPLIT:]

    def transposed(lhs, upstream):
        return lax.dot_general(
            lhs, upstream, (((0,), (0,)), ((), ())), preferred_element_type=F32
        )

    def rest_term(first, number, upstream):
        return transposed(rest_all[:, first * rows : (first + number) * rows], upstream)

    a_far1, a_far0, b_far = line.step(
        transposed(far_all[:, rows:], up_a).astype(BF),
        transposed(far_all[:, :rows], up_a).astype(BF),
        transposed(far_all[:, rows:], up_b).astype(BF),
    )
    a_far1 = send(a_far1, DOWN)
    a_far0 = send(a_far0, UP)
    b_far = send(b_far, ACROSS)

    where = jnp.concatenate([spots(1 - core, *rest_blocks), spots(core, *rest_blocks)])
    rest_sent, rest_kept = line.step(*split_columns(line.hold(tok), where, rows))
    got_rest = send(rest_sent, SWAP)
    got_rest = line.step(got_rest)
    rest_all = line.step(fill_lower(got_rest, rest_kept))
    b_rest = line.step(rest_term(1, 3, up_b).astype(BF))
    b_rest = send(b_rest, ACROSS)
    a_one = line.step(rest_term(0, 2, up_a))
    share = line.step(share)
    share_other = lax.ppermute(share, "island", X_LO)
    a_three = line.step(rest_term(3, 2, up_a))
    b_two = line.step(transposed(far_all[:, :rows], up_b))

    a_far0, a_far1, b_far = line.step(a_far0, a_far1, b_far)
    up_sent = jnp.concatenate([a_one[:rows] + wide(a_far0), a_one[rows:]]).astype(BF)
    down_sent = jnp.concatenate([a_three[:rows] + wide(a_far1), a_three[rows:]]).astype(BF)
    b_low, b_high = (
        (b_two[:half] + wide(b_far[:half])).astype(BF),
        (b_two[half:] + wide(b_far[half:])).astype(BF),
    )
    up_sent, down_sent, b_low, b_high = line.step(up_sent, down_sent, b_low, b_high)
    from_down, from_up = send(up_sent, UP), send(down_sent, DOWN)
    b_low, b_high = send(b_low, UP), send(b_high, DOWN)
    share_other, rest_all = line.step(share_other, rest_all)
    b_one, b_three = line.step(rest_term(0, 1, up_b), rest_term(4, 2, up_b))

    from_down, from_up, rest_all, share_other = line.step(from_down, from_up, rest_all, share_other)
    a_side = rest_term(2, 1, up_a) + wide(from_down[rows:]) + wide(from_up[:rows])
    a_side = line.step(a_side.astype(BF))
    a_side = send(a_side, ACROSS)
    share, rest_all = line.step(share + share_other, rest_all)
    total = lax.all_gather(share, "island", axis=0, axis_index_groups=Z_GROUPS, tiled=True)
    from_down, from_up = line.hold(from_down, from_up)
    a_here = rest_term(5, 1, up_a) + wide(from_down[:rows]) + wide(from_up[rows:])
    a_here = line.step(a_here)

    b_rest, b_low, b_high = line.step(b_rest, b_low, b_high)
    b_up = b_one + wide(b_rest[:rows])
    b_here = b_three[rows:] + wide(b_rest[rows : 2 * rows])
    b_down = b_three[:rows] + wide(b_rest[2 * rows :])
    b_up = jnp.concatenate([b_up[:half] + wide(b_low), b_up[half:]]).astype(BF)
    b_down = jnp.concatenate([b_down[:half], b_down[half:] + wide(b_high)]).astype(BF)
    b_up, b_down, b_here = line.step(b_up, b_down, b_here)
    b_up, b_down = send(b_up, UP), send(b_down, DOWN)

    def inner_update(grad, part):
        master = key_master[0][:, part]
        first_new = BETA_ONE * key_first[0][:, part] + (1.0 - BETA_ONE) * grad
        second_new = BETA_TWO * key_second[0][:, part] + (1.0 - BETA_TWO) * grad * grad
        update = first_new / (jnp.sqrt(second_new) + EPSILON)
        master_new = master - INNER_RATE * (update + DECAY_RATE * master)
        return master_new, first_new, second_new

    a_side, b_up, b_down = line.step(a_side, b_up, b_down)
    grad = jnp.concatenate(
        [a_here + wide(a_side), b_here + wide(b_up) + wide(b_down)], axis=1
    )
    w, grad = line.step(inner_update(grad, slice(None))[0].astype(BF), grad)
    w_dn, w_up, w_x = send(w, UP), send(w, DOWN), send(w, ACROSS)
    states = line.step(*inner_update(grad, slice(None)))
    total, momentum_rows = line.step(total, frag_momentum)
    outer_grad = total / N_ISLAND
    new_momentum = OUTER_MOMENT * momentum_rows + outer_grad
    new_anchor = frag_anchor - OUTER_RATE * (outer_grad + OUTER_MOMENT * new_momentum)
    new_anchor, new_momentum = line.step(new_anchor, new_momentum)

    w_dn, w_up, w_x = line.step(w_dn, w_up, w_x)
    other, near, low, high = line.step(*gather_pieces(w_up, w_dn, w_x))
    near_x = send(near, ACROSS)
    low, high = send(low, UP), send(high, DOWN)
    o_dn, o_up = send(other, UP), send(other, DOWN)
    at = rest_blocks.index
    rest_late = line.hold(rest_all)
    keys = line.step(
        keys_call(
            rows,
            0,
            2 * count,
            [
                ((rest_late, at(b)), (v,))
                for b, v in (((1, 0), w_up), ((3, 0), w_dn), ((0, 0), w), ((0, 1), w_x))
            ],
        )
    )

    near_x, low, high, o_dn, o_up = line.step(near_x, low, high, o_dn, o_up)
    far_low, far_high = low, high
    far_b = jnp.concatenate([low[:, SPLIT:], high[:, SPLIT:]])
    far_b, low, high = line.step(far_b, o_dn[:half], o_up[half:])
    far_x = send(far_b, ACROSS)
    low, high = send(low, UP), send(high, DOWN)
    rest_late, far_low, far_high = line.hold(rest_all, far_low, far_high)
    w_far = jnp.concatenate([far_low, far_high])
    keys = line.step(
        keys_call(
            rows,
            0,
            2 * count,
            [
                ((rest_late, at((1, 1))), (o_up, near_x[:rows])),
                ((rest_late, at((3, 1))), (o_dn, near_x[rows:])),
                ((far_all, 0), (w_far,)),
            ],
            keys,
        )
    )
    far_x, low, high = line.step(far_x, low, high)
    last = [((far_all, 1), (jnp.concatenate([low, high]), far_x))]
    part = line.step(keys_call(rows, count, count, last, keys))
    part = send(part, SWAP)
    mine = keys_call(rows, 0, count, last, keys)
    return (*(v[None] for v in states), (mine + part)[None], new_anchor, new_momentum)


def solution(mesh):
    whole = P("island", "fsdp", None)
    flat = P("fsdp", None)
    return jax.shard_map(
        per_device,
        mesh=mesh,
        in_specs=(whole,) * 6 + (flat, flat),
        out_specs=(whole,) * 4 + (flat, flat),
        check_vma=False,
    )
```
